32 devices in a mesh: beam: 2 (over y), inp: 8 (over z, x), span: 2 (over core).
Axes of the slice: x: 2, y: 2, z: 4, core: 2. Of those that a mesh axis runs over, the one named last changes fastest.
Arguments:
- voltages: bfloat16 [2, 8, 1024, 16384], P(None, 'beam', 'inp', 'span'), parts along dimension 1, may hold values from -6 to 6
- gains: float32 [2, 8, 1024, 32], P(None, 'beam', 'inp'), parts along dimension 1, may hold values from -4 to 4
Outputs:
- visibilities: bfloat16 [256, 1024, 1024], P(('beam', 'inp'), 'span'), parts along dimension 0
The draws below stay inside these ranges and needn't reach their ends.
There are 2 independent parts, one for each index of `beam`. The reference program is written for one: setup_inputs(seed, part) draws one part's arguments, and reference() takes and returns one part's arrays. A program takes and returns all parts, laid end to end along the dimension named above; each array names one. Nothing has to cross between parts.
All inputs are finite; a program needn't handle non-finite values.
Results may differ from the reference program's by a relative error of at most 0.0085.
Values may be sent and summed in bfloat16 or wider, within the bound.
A program may use at most 192 MiB of HBM per device.

```python
import math
import jax
import jax.numpy as jnp
from jax import lax

NI = 1024
FINE = 32
TAPS = 4
COARSE = 4
FRAMES = 256
SAMPLES = 8192
SPANS = 2


def shard_levels(own_key, shape, split, low, high):
    def one(dim, shards_of):
        draws = jax.random.uniform(jax.random.fold_in(jax.random.fold_in(own_key, 6), dim), (shards_of,), jnp.float32, low / len(split), high / len(split))
        return jnp.repeat(jnp.exp(draws), shape[dim] // shards_of).reshape((-1,) + (1,) * (len(shape) - dim - 1))

    level = one(*split[0])
    for cut in split[1:]:
        level = level * one(*cut)
    return level


def bell_draw(own_key, extent, spread, most, pieces=(), held_as=jnp.bfloat16):
    values = spread * jax.random.normal(own_key, extent, jnp.float32)
    if pieces:
        values = values * shard_levels(own_key, extent, pieces, -0.22, 0.18)
    return jnp.clip(values, -most, most).astype(held_as)


def setup_inputs(seed: int = 0, part: int = 0) -> dict:
    key_list = jax.random.split(jax.random.key(seed), 3)
    own_keys = jax.random.split(jax.random.fold_in(key_list[2], part), 3)
    return {
        "voltages": bell_draw(own_keys[0], (2, COARSE, NI, SPANS * SAMPLES), 1.0, 6.0, ((2, 8), (3, 2))),
        "gains": bell_draw(own_keys[1], (2, COARSE, NI, FINE), 0.7, 4.0, ((2, 8),), jnp.float32),
    }


def prototype(tap_count, fine_count):
    length = tap_count * fine_count
    offsets = jnp.arange(length).astype(jnp.float32)
    shifted = (offsets - length / 2 + 0.5) / fine_count
    taper = 0.5 - 0.5 * jnp.cos(2.0 * math.pi * (offsets + 0.5) / length)
    window = jnp.sinc(shifted) * taper
    window = window / jnp.sqrt(jnp.sum(window * window))
    return window.reshape(tap_count, fine_count)

def kernels(window, fine_count):
    points = jnp.arange(fine_count)
    phase_steps = points[:, None] * points[None, :] % fine_count
    angles = 2.0 * math.pi * phase_steps.astype(jnp.float32) / fine_count
    cosine = jnp.cos(angles)
    sine_part = jnp.sin(angles)
    result = []
    for tap_index in range(window.shape[0]):
        weights = window[tap_index][:, None]
        hcos = weights * cosine
        hsin = weights * sine_part
        result.append(jnp.stack([jnp.stack([hcos, -hsin]), jnp.stack([hsin, hcos])]))
    return jnp.stack(result)

def reference(voltages, gains):
    window = prototype(TAPS, FINE)
    filters = kernels(window, FINE)
    frame_scale = 1.0 / (SPANS * FRAMES)

    def one_coarse(coarse_args):
        voltage_block, gain_block = coarse_args
        wide = voltage_block.astype(jnp.float32).reshape(2, NI, SPANS, SAMPLES)
        wide = jnp.pad(wide, ((0, 0), (0, 0), (0, 0), (0, (TAPS - 1) * FINE)))
        spectra = jnp.zeros((2, FINE, NI, SPANS, FRAMES), jnp.float32)
        for tap_index in range(TAPS):
            sample_piece = wide[..., tap_index * FINE:tap_index * FINE + SAMPLES]
            sample_piece = sample_piece.reshape(2, NI, SPANS, FRAMES, FINE)
            spectra = spectra + jnp.einsum('aismp,abpk->bkism', sample_piece, filters[tap_index], precision=lax.Precision.HIGHEST)
        gain_real = gain_block[0].T[:, :, None, None]
        gain_imag = gain_block[1].T[:, :, None, None]
        real_part = spectra[0] * gain_real - spectra[1] * gain_imag
        imag_part = spectra[0] * gain_imag + spectra[1] * gain_real
        return jnp.stack([real_part, imag_part]).astype(jnp.bfloat16).reshape(2, FINE, NI, SPANS * FRAMES)
    spectra_all = lax.map(one_coarse, (jnp.moveaxis(voltages, 1, 0), jnp.moveaxis(gains, 1, 0)))
    channel_data = jnp.moveaxis(spectra_all, 1, 2).reshape(COARSE * FINE, 2, NI, SPANS * FRAMES)
    row_index = jnp.arange(NI)
    upper = row_index[:, None] <= row_index[None, :]

    def one_channel(channel_spec):
        left_rows = jnp.concatenate([channel_spec[0], channel_spec[1]], axis=-1)
        right_rows = jnp.concatenate([channel_spec[1], -channel_spec[0]], axis=-1)
        real_sums = jnp.dot(left_rows, left_rows.T, preferred_element_type=jnp.float32)
        imag_sums = jnp.dot(right_rows, left_rows.T, preferred_element_type=jnp.float32)
        return jnp.where(upper, real_sums * frame_scale, imag_sums * frame_scale).astype(jnp.bfloat16)
    return lax.map(one_channel, channel_data)
```

```python
import functools
import math

import jax
import jax.numpy as jnp
import numpy as np
from jax import lax
from jax.experimental import pallas as pl
from jax.experimental.pallas import tpu as pltpu
from jax.sharding import PartitionSpec as P

FINE = 32
TAPS = 4
MESH = pl.DeviceIdType.MESH


def prototype(tap_count, fine_count):
    length = tap_count * fine_count
    offsets = jnp.arange(length).astype(jnp.float32)
    shifted = (offsets - length / 2 + 0.5) / fine_count
    taper = 0.5 - 0.5 * jnp.cos(2.0 * math.pi * (offsets + 0.5) / length)
    window = jnp.sinc(shifted) * taper
    window = window / jnp.sqrt(jnp.sum(window * window))
    return window.reshape(tap_count, fine_count)


def kernels(window, fine_count):
    points = jnp.arange(fine_count)
    phase_steps = points[:, None] * points[None, :] % fine_count
    angles = 2.0 * math.pi * phase_steps.astype(jnp.float32) / fine_count
    cosine = jnp.cos(angles)
    sine_part = jnp.sin(angles)
    result = []
    for tap_index in range(window.shape[0]):
        weights = window[tap_index][:, None]
        hcos = weights * cosine
        hsin = weights * sine_part
        result.append(jnp.stack([jnp.stack([hcos, -hsin]), jnp.stack([hsin, hcos])]))
    return jnp.stack(result)


def packed_rows(left_rows, right_rows, left_all, row_start):
    real_sums = jnp.einsum("cif,cjf->cij", left_rows, left_all, preferred_element_type=jnp.float32)
    imag_sums = jnp.einsum("cif,cjf->cij", right_rows, left_all, preferred_element_type=jnp.float32)
    row_index = row_start + jnp.arange(left_rows.shape[1])
    col_index = jnp.arange(left_all.shape[1])
    upper = row_index[:, None] <= col_index[None, :]
    return jnp.where(upper[None], real_sums, imag_sums)


def local(voltages, gains):
    coarse = voltages.shape[1]
    local_inputs = voltages.shape[2]
    samples = voltages.shape[3]
    frames = samples // FINE
    window = prototype(TAPS, FINE)
    filters = kernels(window, FINE)
    filter_table = jnp.transpose(filters, (1, 0, 3, 2, 4))
    filter_high = filter_table.astype(jnp.bfloat16)
    filter_low = (filter_table - filter_high.astype(jnp.float32)).astype(jnp.bfloat16)
    padded = jnp.pad(voltages, ((0, 0), (0, 0), (0, 0), (0, (TAPS - 1) * FINE)))
    stacked = jnp.stack(
        [padded[..., tap_index * FINE : tap_index * FINE + samples] for tap_index in range(TAPS)],
        axis=1,
    )
    stacked = stacked.reshape(2, TAPS, coarse, local_inputs, frames, FINE)
    spectra = jnp.einsum(
        "atcnmp,atpbk->bcknm", stacked, filter_high, preferred_element_type=jnp.float32
    )
    spectra = spectra + jnp.einsum(
        "atcnmp,atpbk->bcknm", stacked, filter_low, preferred_element_type=jnp.float32
    )
    gain_real = jnp.swapaxes(gains[0], 1, 2)[:, :, :, None]
    gain_imag = jnp.swapaxes(gains[1], 1, 2)[:, :, :, None]
    real_part = spectra[0] * gain_real - spectra[1] * gain_imag
    imag_part = spectra[0] * gain_imag + spectra[1] * gain_real
    outgoing = jnp.stack([real_part, imag_part]).astype(jnp.bfloat16)
    outgoing = outgoing.reshape(2, coarse * FINE, local_inputs, frames)
    turned = lax.all_to_all(outgoing, "inp", split_axis=1, concat_axis=2, tiled=True)
    inputs = turned.shape[2]
    span_count = lax.axis_size("span")
    row_count = inputs // span_count
    frame_scale = 1.0 / (span_count * frames)
    row_start = lax.axis_index("span") * row_count
    frame_piece = lax.all_gather(turned, "span", axis=3, tiled=True)
    left_all = jnp.concatenate([frame_piece[0], frame_piece[1]], axis=-1)
    own_rows = lax.dynamic_slice_in_dim(frame_piece, row_start, row_count, 2)
    left_rows = jnp.concatenate([own_rows[0], own_rows[1]], axis=-1)
    right_rows = jnp.concatenate([own_rows[1], -own_rows[0]], axis=-1)
    summed = packed_rows(left_rows, right_rows, left_all, row_start) * frame_scale
    return summed.astype(jnp.bfloat16)


def order_of(step, mine, coarse):
    if coarse == 4:
        high = (mine // 2 + 1 - step // 2) % 2
        low = (mine % 2 + (step + 1) // 2) % 2
        return 2 * high + low
    return (mine + step + 1) % coarse


def filter_rows(fine_count, tap_count, group):
    length = tap_count * fine_count
    offsets = np.arange(length, dtype=np.float64)
    shifted = (offsets - length / 2 + 0.5) / fine_count
    taper = 0.5 - 0.5 * np.cos(2.0 * np.pi * (offsets + 0.5) / length)
    window = np.sinc(shifted) * taper
    window = window / np.sqrt(np.sum(window * window))
    fine = np.arange(fine_count)
    angles = 2.0 * np.pi * ((offsets[None, :] * fine[:, None]) % fine_count) / fine_count
    hcos = window[None, :] * np.cos(angles)
    hsin = window[None, :] * np.sin(angles)
    span = group * fine_count + length
    rows = np.zeros((group, 2, fine_count, 2, span), np.float64)
    for frame in range(group):
        at = slice(frame * fine_count, frame * fine_count + length)
        rows[frame, 0, :, 0, at] = hcos
        rows[frame, 0, :, 1, at] = hsin
        rows[frame, 1, :, 0, at] = -hsin
        rows[frame, 1, :, 1, at] = hcos
    rows = rows.reshape(group * 2 * fine_count, 2 * span).astype(np.float32)
    high = rows.astype(jnp.bfloat16)
    low = (rows - high.astype(np.float32)).astype(jnp.bfloat16)
    return high, low


def fused_kernel(
    dims, volt, gains, high, low, vis, send, recv,
    xbuf, tbuf, stage, bbuf, lefts, rights, obuf,
    xsem, stsem, ssem, rsem, psend, precv, bsem, osem,
):
    ranks, coarse, chunks, each, local_inputs, frames, scale = dims
    halves = ranks // coarse
    samples = frames * FINE
    rows = ranks * local_inputs // 2
    ahead = min(4, chunks)
    early = min(2, chunks)
    beam = lax.axis_index("beam")
    me = lax.axis_index("inp")
    span = lax.axis_index("span")
    mine = me // halves
    my_half = me % halves

    def peer(step, turn):
        return order_of(step, mine, coarse) * halves + (my_half + turn) % halves

    peers = [(step, turn) for step in range(coarse) for turn in range(halves)]
    peers = [pair for pair in peers if pair != (coarse - 1, 0)]

    barrier = pltpu.get_barrier_semaphore()
    for step, turn in peers:
        pl.semaphore_signal(barrier, inc=1, device_id=(beam, peer(step, turn), span), device_id_type=MESH)
    pl.semaphore_signal(barrier, inc=1, device_id=(beam, me, 1 - span), device_id_type=MESH)
    pl.semaphore_wait(barrier, len(peers) + 1)

    def load(step, slot):
        block = order_of(step, mine, coarse)
        return pltpu.make_async_copy(
            volt.at[:, block], xbuf.at[slot, :, :, pl.ds(0, samples)], xsem.at[slot]
        )

    def outgoing(step, turn, chunk):
        other = peer(step, turn)
        return pltpu.make_async_remote_copy(
            src_ref=send.at[other, chunk],
            dst_ref=recv.at[span, chunk, me],
            send_sem=ssem.at[chunk, other],
            recv_sem=rsem.at[chunk, me],
            device_id=(beam, other, span),
            device_id_type=MESH,
        )

    def incoming(step, turn, chunk):
        other = peer(step, turn)
        return pltpu.make_async_remote_copy(
            src_ref=send.at[other, chunk],
            dst_ref=recv.at[span, chunk, other],
            send_sem=ssem.at[chunk, other],
            recv_sem=rsem.at[chunk, other],
            device_id=(beam, other, span),
            device_id_type=MESH,
        )

    def forward(chunk):
        return pltpu.make_async_remote_copy(
            src_ref=recv.at[span, chunk],
            dst_ref=recv.at[span, chunk],
            send_sem=psend.at[chunk],
            recv_sem=precv.at[chunk],
            device_id=(beam, me, 1 - span),
            device_id_type=MESH,
        )

    def backward(chunk):
        return pltpu.make_async_remote_copy(
            src_ref=recv.at[1 - span, chunk],
            dst_ref=recv.at[1 - span, chunk],
            send_sem=psend.at[chunk],
            recv_sem=precv.at[chunk],
            device_id=(beam, me, 1 - span),
            device_id_type=MESH,
        )

    tail = jnp.zeros((2, local_inputs, TAPS * FINE), jnp.bfloat16)
    xbuf[0, :, :, pl.ds(samples, TAPS * FINE)] = tail
    xbuf[1, :, :, pl.ds(samples, TAPS * FINE)] = tail

    def channelize(step, slot):
        block = order_of(step, mine, coarse)
        load(step, slot).wait()

        @pl.loop(0, frames // 8)
        def _(pair):
            base = pl.multiple_of(pair * (8 * FINE), 4 * FINE)
            pieces = []
            for part in range(2):
                at = base + part * 4 * FINE
                at = pl.multiple_of(at, 4 * FINE)
                pieces.append(
                    jnp.concatenate(
                        [xbuf[slot, 0, :, pl.ds(at, 8 * FINE)], xbuf[slot, 1, :, pl.ds(at, 8 * FINE)]],
                        axis=1,
                    )
                )
            both = jnp.concatenate(pieces, axis=0)
            contract = (((1,), (1,)), ((), ()))
            got = lax.dot_general(high[...], both, contract, preferred_element_type=jnp.float32)
            got = got + lax.dot_general(low[...], both, contract, preferred_element_type=jnp.float32)
            at = pl.multiple_of(pair * (16 * FINE), 16 * FINE)
            tbuf[pl.ds(at, 8 * FINE), :] = got[:, :local_inputs]
            tbuf[pl.ds(at + 8 * FINE, 8 * FINE), :] = got[:, local_inputs:]

        @pl.loop(0, FINE)
        def _(fine):
            half = fine // (chunks * each)
            chunk = (fine // each) % chunks
            index = fine % each
            real = tbuf[pl.ds(fine, frames, stride=2 * FINE), :]
            imag = tbuf[pl.ds(FINE + fine, frames, stride=2 * FINE), :]
            gain_real = gains[block, 0, pl.ds(fine, 1), :]
            gain_imag = gains[block, 1, pl.ds(fine, 1), :]
            stage[half, chunk, index, 0] = (real * gain_real - imag * gain_imag).astype(jnp.bfloat16)
            stage[half, chunk, index, 1] = (real * gain_imag + imag * gain_real).astype(jnp.bfloat16)

    def put(step, turn):
        half = (my_half + turn) % halves
        if (step, turn) == (coarse - 1, 0):
            return pltpu.make_async_copy(stage.at[half], recv.at[span, :, me], stsem.at[turn])
        return pltpu.make_async_copy(stage.at[half], send.at[peer(step, turn)], stsem.at[turn])

    load(0, 0).start()
    for step in range(coarse):
        if step + 1 < coarse:
            load(step + 1, (step + 1) % 2).start()
        channelize(step, step % 2)
        for turn in range(halves):
            put(step, turn).start()
        for turn in range(halves):
            put(step, turn).wait()
        for chunk in range(early):
            for turn in range(halves):
                if (step, turn) in peers:
                    outgoing(step, turn, chunk).start()
    for chunk in range(early, ahead):
        for step, turn in peers:
            outgoing(step, turn, chunk).start()

    def fetch(chunk, index, part):
        return pltpu.make_async_copy(
            recv.at[part, chunk, :, index], bbuf.at[index, part], bsem.at[index, part]
        )

    def result(chunk, index):
        return pltpu.make_async_copy(obuf.at[index], vis.at[chunk * each + index], osem.at[index])

    own_sources = ranks // 2
    depth = 2 * frames

    def correlate(chunk):
        backward(chunk).wait_recv()
        for index in range(each):
            for part in range(2):
                fetch(chunk, index, part).start()
        for index in range(each):
            for part in range(2):
                fetch(chunk, index, part).wait()

            @pl.loop(0, own_sources)
            def _(source):
                at = pl.multiple_of(source * local_inputs, local_inputs)
                for part in range(2):
                    where_real = pl.ds(part * frames, frames)
                    where_imag = pl.ds(depth + part * frames, frames)
                    real = bbuf[index, part, span * own_sources + source, 0].T
                    imag = bbuf[index, part, span * own_sources + source, 1].T
                    lefts[pl.ds(at, local_inputs), where_real] = real
                    lefts[pl.ds(at, local_inputs), where_imag] = imag
                    rights[pl.ds(at, local_inputs), where_real] = imag
                    rights[pl.ds(at, local_inputs), where_imag] = -real

            @pl.loop(0, ranks // 2)
            def _(pair):
                columns = []
                for side in range(2):
                    source = pair * 2 + side
                    columns.append(
                        jnp.concatenate(
                            [bbuf[index, part, source, piece] for piece in range(2) for part in range(2)],
                            axis=0,
                        )
                    )
                block = jnp.concatenate(columns, axis=1)
                width = 2 * local_inputs
                real = jnp.dot(lefts[...], block, preferred_element_type=jnp.float32)
                imag = jnp.dot(rights[...], block, preferred_element_type=jnp.float32)
                row = span * rows + lax.broadcasted_iota(jnp.int32, (rows, width), 0)
                column = pair * width + lax.broadcasted_iota(jnp.int32, (rows, width), 1)
                value = jnp.where(row <= column, real, imag) * scale
                at = pl.multiple_of(pair * width, width)
                obuf[index, :, pl.ds(at, width)] = value.astype(jnp.bfloat16)

            result(chunk, index).start()
        for index in range(each):
            result(chunk, index).wait()

    @pl.loop(0, chunks)
    def _(chunk):
        for step, turn in peers:
            incoming(step, turn, chunk).wait_recv()
        forward(chunk).start()

        @pl.when(chunk + ahead < chunks)
        def _():
            for step, turn in peers:
                outgoing(step, turn, chunk + ahead).start()

        @pl.when(chunk > 0)
        def _():
            correlate(chunk - 1)

    correlate(chunks - 1)

    @pl.loop(0, chunks)
    def _(chunk):
        for step, turn in peers:
            outgoing(step, turn, chunk).wait_send()
        forward(chunk).wait_send()


def fused(voltages, gains):
    coarse, local_inputs, samples = voltages.shape[1:]
    ranks = lax.axis_size("inp")
    frames = samples // FINE
    halves = ranks // coarse
    owned = FINE // halves
    each = 2
    chunks = owned // each
    rows = ranks * local_inputs // 2
    columns = ranks * local_inputs
    high, low = filter_rows(FINE, TAPS, 4)
    gain_rows = jnp.transpose(gains, (1, 0, 3, 2))
    scale = 1.0 / (2 * frames)
    dims = (ranks, coarse, chunks, each, local_inputs, frames, scale)
    bf16 = jnp.bfloat16
    anywhere = pl.BlockSpec(memory_space=pl.ANY)
    inside = pl.BlockSpec(memory_space=pltpu.VMEM)
    flops = 4 * owned * rows * columns * 4 * frames
    vis, _, _ = pl.pallas_call(
        functools.partial(fused_kernel, dims),
        out_shape=(
            jax.ShapeDtypeStruct((owned, rows, columns), bf16),
            jax.ShapeDtypeStruct((ranks, chunks, each, 2, frames, local_inputs), bf16),
            jax.ShapeDtypeStruct((2, chunks, ranks, each, 2, frames, local_inputs), bf16),
        ),
        in_specs=[anywhere, inside, inside, inside],
        out_specs=(anywhere, anywhere, anywhere),
        scratch_shapes=[
            pltpu.VMEM((2, 2, local_inputs, samples + TAPS * FINE), bf16),
            pltpu.VMEM((frames * 2 * FINE, local_inputs), jnp.float32),
            pltpu.VMEM((halves, chunks, each, 2, frames, local_inputs), bf16),
            pltpu.VMEM((each, 2, ranks, 2, frames, local_inputs), bf16),
            pltpu.VMEM((rows, 4 * frames), bf16),
            pltpu.VMEM((rows, 4 * frames), bf16),
            pltpu.VMEM((each, rows, columns), bf16),
            pltpu.SemaphoreType.DMA((2,)),
            pltpu.SemaphoreType.DMA((halves,)),
            pltpu.SemaphoreType.DMA((chunks, ranks)),
            pltpu.SemaphoreType.DMA((chunks, ranks)),
            pltpu.SemaphoreType.DMA((chunks,)),
            pltpu.SemaphoreType.DMA((chunks,)),
            pltpu.SemaphoreType.DMA((each, 2)),
            pltpu.SemaphoreType.DMA((each,)),
        ],
        compiler_params=pltpu.CompilerParams(
            collective_id=0, has_side_effects=True, vmem_limit_bytes=60 * 1024 * 1024
        ),
        cost_estimate=pl.CostEstimate(flops=flops, bytes_accessed=2 * voltages.size * 8, transcendentals=0),
    )(voltages, gain_rows, jnp.asarray(high), jnp.asarray(low))
    return vis


def chosen(voltages, gains):
    coarse, local_inputs, samples = voltages.shape[1:]
    ranks, spans = lax.axis_size("inp"), lax.axis_size("span")
    fits = (
        spans == 2
        and local_inputs % 128 == 0
        and ranks % coarse == 0
        and ranks % 2 == 0
        and FINE % (2 * (ranks // coarse)) == 0
        and samples % (16 * FINE) == 0
    )
    return fused(voltages, gains) if fits else local(voltages, gains)


def solution(mesh):
    placed = (P(None, "beam", "inp", "span"), P(None, "beam", "inp", None))
    return jax.shard_map(
        chosen,
        mesh=mesh,
        in_specs=placed,
        out_specs=P(("beam", "inp"), "span", None),
        check_vma=False,
    )
```

```python
import functools
import math

import jax
import jax.numpy as jnp
import numpy as np
from jax import lax
from jax.experimental import pallas as pl
from jax.experimental.pallas import tpu as pltpu
from jax.sharding import PartitionSpec as P

FINE = 32
TAPS = 4
MESH = pl.DeviceIdType.MESH


def prototype(tap_count, fine_count):
    length = tap_count * fine_count
    offsets = jnp.arange(length).astype(jnp.float32)
    shifted = (offsets - length / 2 + 0.5) / fine_count
    taper = 0.5 - 0.5 * jnp.cos(2.0 * math.pi * (offsets + 0.5) / length)
    window = jnp.sinc(shifted) * taper
    window = window / jnp.sqrt(jnp.sum(window * window))
    return window.reshape(tap_count, fine_count)


def kernels(window, fine_count):
    points = jnp.arange(fine_count)
    phase_steps = points[:, None] * points[None, :] % fine_count
    angles = 2.0 * math.pi * phase_steps.astype(jnp.float32) / fine_count
    cosine = jnp.cos(angles)
    sine_part = jnp.sin(angles)
    result = []
    for tap_index in range(window.shape[0]):
        weights = window[tap_index][:, None]
        hcos = weights * cosine
        hsin = weights * sine_part
        result.append(jnp.stack([jnp.stack([hcos, -hsin]), jnp.stack([hsin, hcos])]))
    return jnp.stack(result)


def packed_rows(left_rows, right_rows, left_all, row_start):
    real_sums = jnp.einsum("cif,cjf->cij", left_rows, left_all, preferred_element_type=jnp.float32)
    imag_sums = jnp.einsum("cif,cjf->cij", right_rows, left_all, preferred_element_type=jnp.float32)
    row_index = row_start + jnp.arange(left_rows.shape[1])
    col_index = jnp.arange(left_all.shape[1])
    upper = row_index[:, None] <= col_index[None, :]
    return jnp.where(upper[None], real_sums, imag_sums)


def local(voltages, gains):
    coarse = voltages.shape[1]
    local_inputs = voltages.shape[2]
    samples = voltages.shape[3]
    frames = samples // FINE
    window = prototype(TAPS, FINE)
    filters = kernels(window, FINE)
    filter_table = jnp.transpose(filters, (1, 0, 3, 2, 4))
    filter_high = filter_table.astype(jnp.bfloat16)
    filter_low = (filter_table - filter_high.astype(jnp.float32)).astype(jnp.bfloat16)
    padded = jnp.pad(voltages, ((0, 0), (0, 0), (0, 0), (0, (TAPS - 1) * FINE)))
    stacked = jnp.stack(
        [padded[..., tap_index * FINE : tap_index * FINE + samples] for tap_index in range(TAPS)],
        axis=1,
    )
    stacked = stacked.reshape(2, TAPS, coarse, local_inputs, frames, FINE)
    spectra = jnp.einsum(
        "atcnmp,atpbk->bcknm", stacked, filter_high, preferred_element_type=jnp.float32
    )
    spectra = spectra + jnp.einsum(
        "atcnmp,atpbk->bcknm", stacked, filter_low, preferred_element_type=jnp.float32
    )
    gain_real = jnp.swapaxes(gains[0], 1, 2)[:, :, :, None]
    gain_imag = jnp.swapaxes(gains[1], 1, 2)[:, :, :, None]
    real_part = spectra[0] * gain_real - spectra[1] * gain_imag
    imag_part = spectra[0] * gain_imag + spectra[1] * gain_real
    outgoing = jnp.stack([real_part, imag_part]).astype(jnp.bfloat16)
    outgoing = outgoing.reshape(2, coarse * FINE, local_inputs, frames)
    turned = lax.all_to_all(outgoing, "inp", split_axis=1, concat_axis=2, tiled=True)
    inputs = turned.shape[2]
    span_count = lax.axis_size("span")
    row_count = inputs // span_count
    frame_scale = 1.0 / (span_count * frames)
    row_start = lax.axis_index("span") * row_count
    frame_piece = lax.all_gather(turned, "span", axis=3, tiled=True)
    left_all = jnp.concatenate([frame_piece[0], frame_piece[1]], axis=-1)
    own_rows = lax.dynamic_slice_in_dim(frame_piece, row_start, row_count, 2)
    left_rows = jnp.concatenate([own_rows[0], own_rows[1]], axis=-1)
    right_rows = jnp.concatenate([own_rows[1], -own_rows[0]], axis=-1)
    summed = packed_rows(left_rows, right_rows, left_all, row_start) * frame_scale
    return summed.astype(jnp.bfloat16)


def order_of(step, mine, coarse):
    if coarse == 4:
        high = (mine // 2 + 1 - step // 2) % 2
        low = (mine % 2 + (step + 1) // 2) % 2
        return 2 * high + low
    return (mine + step + 1) % coarse


def filter_rows(fine_count, tap_count, group):
    length = tap_count * fine_count
    offsets = np.arange(length, dtype=np.float64)
    shifted = (offsets - length / 2 + 0.5) / fine_count
    taper = 0.5 - 0.5 * np.cos(2.0 * np.pi * (offsets + 0.5) / length)
    window = np.sinc(shifted) * taper
    window = window / np.sqrt(np.sum(window * window))
    fine = np.arange(fine_count)
    angles = 2.0 * np.pi * ((offsets[None, :] * fine[:, None]) % fine_count) / fine_count
    hcos = window[None, :] * np.cos(angles)
    hsin = window[None, :] * np.sin(angles)
    span = group * fine_count + length
    rows = np.zeros((group, 2, fine_count, 2, span), np.float64)
    for frame in range(group):
        at = slice(frame * fine_count, frame * fine_count + length)
        rows[frame, 0, :, 0, at] = hcos
        rows[frame, 0, :, 1, at] = hsin
        rows[frame, 1, :, 0, at] = -hsin
        rows[frame, 1, :, 1, at] = hcos
    rows = rows.reshape(group * 2 * fine_count, 2 * span).astype(np.float32)
    high = rows.astype(jnp.bfloat16)
    low = (rows - high.astype(np.float32)).astype(jnp.bfloat16)
    return high, low


def fused_kernel(
    dims, volt, gains, high, low, vis, send, recv,
    xbuf, tbuf, stage, bbuf, turned, obuf,
    xsem, stsem, ssem, rsem, psend, precv, bsem, osem,
):
    ranks, coarse, chunks, each, local_inputs, frames, scale = dims
    halves = ranks // coarse
    samples = frames * FINE
    rows = ranks * local_inputs // 2
    ahead = min(8, chunks)
    early = min(4, chunks)
    beam = lax.axis_index("beam")
    me = lax.axis_index("inp")
    span = lax.axis_index("span")
    mine = me // halves
    my_half = me % halves

    def peer(step, turn):
        return order_of(step, mine, coarse) * halves + (my_half + turn) % halves

    peers = [(step, turn) for step in range(coarse) for turn in range(halves)]
    peers = [pair for pair in peers if pair != (coarse - 1, 0)]

    barrier = pltpu.get_barrier_semaphore()
    for step, turn in peers:
        pl.semaphore_signal(barrier, inc=1, device_id=(beam, peer(step, turn), span), device_id_type=MESH)
    pl.semaphore_signal(barrier, inc=1, device_id=(beam, me, 1 - span), device_id_type=MESH)
    pl.semaphore_wait(barrier, len(peers) + 1)

    def load(step, slot):
        block = order_of(step, mine, coarse)
        return pltpu.make_async_copy(
            volt.at[:, block], xbuf.at[slot, :, :, pl.ds(0, samples)], xsem.at[slot]
        )

    def outgoing(step, turn, chunk):
        other = peer(step, turn)
        return pltpu.make_async_remote_copy(
            src_ref=send.at[other, chunk],
            dst_ref=recv.at[span, chunk, me],
            send_sem=ssem.at[chunk, other],
            recv_sem=rsem.at[chunk, me],
            device_id=(beam, other, span),
            device_id_type=MESH,
        )

    def incoming(step, turn, chunk):
        other = peer(step, turn)
        return pltpu.make_async_remote_copy(
            src_ref=send.at[other, chunk],
            dst_ref=recv.at[span, chunk, other],
            send_sem=ssem.at[chunk, other],
            recv_sem=rsem.at[chunk, other],
            device_id=(beam, other, span),
            device_id_type=MESH,
        )

    def forward(chunk):
        return pltpu.make_async_remote_copy(
            src_ref=recv.at[span, chunk],
            dst_ref=recv.at[span, chunk],
            send_sem=psend.at[chunk],
            recv_sem=precv.at[chunk],
            device_id=(beam, me, 1 - span),
            device_id_type=MESH,
        )

    def backward(chunk):
        return pltpu.make_async_remote_copy(
            src_ref=recv.at[1 - span, chunk],
            dst_ref=recv.at[1 - span, chunk],
            send_sem=psend.at[chunk],
            recv_sem=precv.at[chunk],
            device_id=(beam, me, 1 - span),
            device_id_type=MESH,
        )

    tail = jnp.zeros((2, local_inputs, TAPS * FINE), jnp.bfloat16)
    xbuf[0, :, :, pl.ds(samples, TAPS * FINE)] = tail
    xbuf[1, :, :, pl.ds(samples, TAPS * FINE)] = tail

    def channelize(step, slot):
        load(step, slot).wait()

        @pl.loop(0, frames // 8, unroll=2)
        def _(pair):
            base = pl.multiple_of(pair * (8 * FINE), 4 * FINE)
            pieces = []
            for part in range(2):
                at = base + part * 4 * FINE
                at = pl.multiple_of(at, 4 * FINE)
                pieces.append(
                    jnp.concatenate(
                        [xbuf[slot, 0, :, pl.ds(at, 8 * FINE)], xbuf[slot, 1, :, pl.ds(at, 8 * FINE)]],
                        axis=1,
                    )
                )
            both = jnp.concatenate(pieces, axis=0)
            contract = (((1,), (1,)), ((), ()))
            got = lax.dot_general(high[...], both, contract, preferred_element_type=jnp.float32)
            got = got + lax.dot_general(low[...], both, contract, preferred_element_type=jnp.float32)
            at = pl.multiple_of(pair * (16 * FINE), 16 * FINE)
            tbuf[pl.ds(at, 8 * FINE), :] = got[:, :local_inputs]
            tbuf[pl.ds(at + 8 * FINE, 8 * FINE), :] = got[:, local_inputs:]

    def weigh(step, turn):
        block = order_of(step, mine, coarse)
        half = (my_half + turn) % halves

        @pl.loop(0, chunks * each, unroll=2)
        def _(own):
            chunk = own // each
            index = own % each
            fine = half * (chunks * each) + own
            real = tbuf[pl.ds(fine, frames, stride=2 * FINE), :]
            imag = tbuf[pl.ds(FINE + fine, frames, stride=2 * FINE), :]
            gain_real = gains[block, 0, pl.ds(fine, 1), :]
            gain_imag = gains[block, 1, pl.ds(fine, 1), :]
            stage[half, chunk, index, 0] = (real * gain_real - imag * gain_imag).astype(jnp.bfloat16)
            stage[half, chunk, index, 1] = (real * gain_imag + imag * gain_real).astype(jnp.bfloat16)

    def put(step, turn):
        half = (my_half + turn) % halves
        if (step, turn) == (coarse - 1, 0):
            return pltpu.make_async_copy(stage.at[half], recv.at[span, :, me], stsem.at[turn])
        return pltpu.make_async_copy(stage.at[half], send.at[peer(step, turn)], stsem.at[turn])

    load(0, 0).start()
    for step in range(coarse):
        if step + 1 < coarse:
            load(step + 1, (step + 1) % 2).start()
        channelize(step, step % 2)
        for turn in range(halves):
            weigh(step, turn)
            put(step, turn).start()
            put(step, turn).wait()
            if (step, turn) in peers:
                for chunk in range(early):
                    outgoing(step, turn, chunk).start()
    for chunk in range(early, ahead):
        for step, turn in peers:
            outgoing(step, turn, chunk).start()

    def fetch(chunk, index, part):
        return pltpu.make_async_copy(
            recv.at[part, chunk, :, index], bbuf.at[index, part], bsem.at[index, part]
        )

    def result(chunk, index):
        return pltpu.make_async_copy(obuf.at[index], vis.at[chunk * each + index], osem.at[index])

    own_sources = ranks // 2
    depth = 2 * frames

    def turn_over(index, part):
        @pl.loop(0, own_sources)
        def _(source):
            at = pl.multiple_of(source * local_inputs, local_inputs)
            where_real = pl.ds(pl.multiple_of(part * frames, frames), frames)
            where_imag = pl.ds(pl.multiple_of(depth + part * frames, frames), frames)
            real = bbuf[index, part, span * own_sources + source, 0].T
            imag = bbuf[index, part, span * own_sources + source, 1].T
            turned[0, pl.ds(at, local_inputs), where_real] = real
            turned[0, pl.ds(at, local_inputs), where_imag] = imag
            turned[1, pl.ds(at, local_inputs), where_real] = imag
            turned[1, pl.ds(at, local_inputs), where_imag] = -real

    width = 2 * local_inputs

    def columns_of(index, pair):
        columns = []
        for side in range(2):
            source = pair * 2 + side
            columns.append(
                jnp.concatenate(
                    [bbuf[index, part, source, piece] for piece in range(2) for part in range(2)],
                    axis=0,
                )
            )
        return jnp.concatenate(columns, axis=1)

    def correlate(chunk):
        for index in range(each):
            fetch(chunk, index, span).start()
        for index in range(each):
            fetch(chunk, index, span).wait()
            turn_over(index, span)
            if index == 0:
                backward(chunk).wait_recv()
            fetch(chunk, index, 1 - span).start()
            fetch(chunk, index, 1 - span).wait()
            turn_over(index, 1 - span)

            @pl.loop(0, ranks // 4)
            def _(step):
                pair = (1 - span) * (ranks // 4) + step
                block = columns_of(index, pair)
                value = jnp.dot(turned[span], block, preferred_element_type=jnp.float32) * scale
                at = pl.multiple_of(pair * width, width)
                obuf[index, :, pl.ds(at, width)] = value.astype(jnp.bfloat16)

            @pl.loop(0, ranks // 4)
            def _(step):
                pair = span * (ranks // 4) + step
                block = columns_of(index, pair)
                real = jnp.dot(turned[0], block, preferred_element_type=jnp.float32)
                imag = jnp.dot(turned[1], block, preferred_element_type=jnp.float32)
                row = lax.broadcasted_iota(jnp.int32, (rows, width), 0)
                column = step * width + lax.broadcasted_iota(jnp.int32, (rows, width), 1)
                value = jnp.where(row <= column, real, imag) * scale
                at = pl.multiple_of(pair * width, width)
                obuf[index, :, pl.ds(at, width)] = value.astype(jnp.bfloat16)

            result(chunk, index).start()
        for index in range(each):
            result(chunk, index).wait()

    @pl.loop(0, chunks)
    def _(chunk):
        for step, turn in peers:
            incoming(step, turn, chunk).wait_recv()
        forward(chunk).start()

        @pl.when(chunk + ahead < chunks)
        def _():
            for step, turn in peers:
                outgoing(step, turn, chunk + ahead).start()

        correlate(chunk)

    @pl.loop(0, chunks)
    def _(chunk):
        for step, turn in peers:
            outgoing(step, turn, chunk).wait_send()
        forward(chunk).wait_send()


def fused(voltages, gains):
    coarse, local_inputs, samples = voltages.shape[1:]
    ranks = lax.axis_size("inp")
    frames = samples // FINE
    halves = ranks // coarse
    owned = FINE // halves
    each = 1
    chunks = owned // each
    rows = ranks * local_inputs // 2
    columns = ranks * local_inputs
    high, low = filter_rows(FINE, TAPS, 4)
    gain_rows = jnp.transpose(gains, (1, 0, 3, 2))
    scale = 1.0 / (2 * frames)
    dims = (ranks, coarse, chunks, each, local_inputs, frames, scale)
    bf16 = jnp.bfloat16
    anywhere = pl.BlockSpec(memory_space=pl.ANY)
    inside = pl.BlockSpec(memory_space=pltpu.VMEM)
    flops = 4 * owned * rows * columns * 4 * frames
    vis, _, _ = pl.pallas_call(
        functools.partial(fused_kernel, dims),
        out_shape=(
            jax.ShapeDtypeStruct((owned, rows, columns), bf16),
            jax.ShapeDtypeStruct((ranks, chunks, each, 2, frames, local_inputs), bf16),
            jax.ShapeDtypeStruct((2, chunks, ranks, each, 2, frames, local_inputs), bf16),
        ),
        in_specs=[anywhere, inside, inside, inside],
        out_specs=(anywhere, anywhere, anywhere),
        scratch_shapes=[
            pltpu.VMEM((2, 2, local_inputs, samples + TAPS * FINE), bf16),
            pltpu.VMEM((frames * 2 * FINE, local_inputs), jnp.float32),
            pltpu.VMEM((halves, chunks, each, 2, frames, local_inputs), bf16),
            pltpu.VMEM((each, 2, ranks, 2, frames, local_inputs), bf16),
            pltpu.VMEM((2, rows, 4 * frames), bf16),
            pltpu.VMEM((each, rows, columns), bf16),
            pltpu.SemaphoreType.DMA((2,)),
            pltpu.SemaphoreType.DMA((halves,)),
            pltpu.SemaphoreType.DMA((chunks, ranks)),
            pltpu.SemaphoreType.DMA((chunks, ranks)),
            pltpu.SemaphoreType.DMA((chunks,)),
            pltpu.SemaphoreType.DMA((chunks,)),
            pltpu.SemaphoreType.DMA((each, 2)),
            pltpu.SemaphoreType.DMA((each,)),
        ],
        compiler_params=pltpu.CompilerParams(
            collective_id=0, has_side_effects=True, vmem_limit_bytes=60 * 1024 * 1024
        ),
        cost_estimate=pl.CostEstimate(flops=flops, bytes_accessed=2 * voltages.size * 8, transcendentals=0),
    )(voltages, gain_rows, jnp.asarray(high), jnp.asarray(low))
    return vis


def chosen(voltages, gains):
    coarse, local_inputs, samples = voltages.shape[1:]
    ranks, spans = lax.axis_size("inp"), lax.axis_size("span")
    fits = (
        spans == 2
        and local_inputs % 128 == 0
        and ranks % coarse == 0
        and ranks % 4 == 0
        and FINE % (ranks // coarse) == 0
        and samples % (16 * FINE) == 0
    )
    return fused(voltages, gains) if fits else local(voltages, gains)


def solution(mesh):
    placed = (P(None, "beam", "inp", "span"), P(None, "beam", "inp", None))
    return jax.shard_map(
        chosen,
        mesh=mesh,
        in_specs=placed,
        out_specs=P(("beam", "inp"), "span", None),
        check_vma=False,
    )
```

```python
import functools
import math

import jax
import jax.numpy as jnp
import numpy as np
from jax import lax
from jax.experimental import pallas as pl
from jax.experimental.pallas import tpu as pltpu
from jax.sharding import PartitionSpec as P

FINE = 32
TAPS = 4
MESH = pl.DeviceIdType.MESH


def prototype(tap_count, fine_count):
    length = tap_count * fine_count
    offsets = jnp.arange(length).astype(jnp.float32)
    shifted = (offsets - length / 2 + 0.5) / fine_count
    taper = 0.5 - 0.5 * jnp.cos(2.0 * math.pi * (offsets + 0.5) / length)
    window = jnp.sinc(shifted) * taper
    window = window / jnp.sqrt(jnp.sum(window * window))
    return window.reshape(tap_count, fine_count)


def kernels(window, fine_count):
    points = jnp.arange(fine_count)
    phase_steps = points[:, None] * points[None, :] % fine_count
    angles = 2.0 * math.pi * phase_steps.astype(jnp.float32) / fine_count
    cosine = jnp.cos(angles)
    sine_part = jnp.sin(angles)
    result = []
    for tap_index in range(window.shape[0]):
        weights = window[tap_index][:, None]
        hcos = weights * cosine
        hsin = weights * sine_part
        result.append(jnp.stack([jnp.stack([hcos, -hsin]), jnp.stack([hsin, hcos])]))
    return jnp.stack(result)


def packed_rows(left_rows, right_rows, left_all, row_start):
    real_sums = jnp.einsum("cif,cjf->cij", left_rows, left_all, preferred_element_type=jnp.float32)
    imag_sums = jnp.einsum("cif,cjf->cij", right_rows, left_all, preferred_element_type=jnp.float32)
    row_index = row_start + jnp.arange(left_rows.shape[1])
    col_index = jnp.arange(left_all.shape[1])
    upper = row_index[:, None] <= col_index[None, :]
    return jnp.where(upper[None], real_sums, imag_sums)


def local(voltages, gains):
    coarse = voltages.shape[1]
    local_inputs = voltages.shape[2]
    samples = voltages.shape[3]
    frames = samples // FINE
    window = prototype(TAPS, FINE)
    filters = kernels(window, FINE)
    filter_table = jnp.transpose(filters, (1, 0, 3, 2, 4))
    filter_high = filter_table.astype(jnp.bfloat16)
    filter_low = (filter_table - filter_high.astype(jnp.float32)).astype(jnp.bfloat16)
    padded = jnp.pad(voltages, ((0, 0), (0, 0), (0, 0), (0, (TAPS - 1) * FINE)))
    stacked = jnp.stack(
        [padded[..., tap_index * FINE : tap_index * FINE + samples] for tap_index in range(TAPS)],
        axis=1,
    )
    stacked = stacked.reshape(2, TAPS, coarse, local_inputs, frames, FINE)
    spectra = jnp.einsum(
        "atcnmp,atpbk->bcknm", stacked, filter_high, preferred_element_type=jnp.float32
    )
    spectra = spectra + jnp.einsum(
        "atcnmp,atpbk->bcknm", stacked, filter_low, preferred_element_type=jnp.float32
    )
    gain_real = jnp.swapaxes(gains[0], 1, 2)[:, :, :, None]
    gain_imag = jnp.swapaxes(gains[1], 1, 2)[:, :, :, None]
    real_part = spectra[0] * gain_real - spectra[1] * gain_imag
    imag_part = spectra[0] * gain_imag + spectra[1] * gain_real
    outgoing = jnp.stack([real_part, imag_part]).astype(jnp.bfloat16)
    outgoing = outgoing.reshape(2, coarse * FINE, local_inputs, frames)
    turned = lax.all_to_all(outgoing, "inp", split_axis=1, concat_axis=2, tiled=True)
    inputs = turned.shape[2]
    span_count = lax.axis_size("span")
    row_count = inputs // span_count
    frame_scale = 1.0 / (span_count * frames)
    row_start = lax.axis_index("span") * row_count
    frame_piece = lax.all_gather(turned, "span", axis=3, tiled=True)
    left_all = jnp.concatenate([frame_piece[0], frame_piece[1]], axis=-1)
    own_rows = lax.dynamic_slice_in_dim(frame_piece, row_start, row_count, 2)
    left_rows = jnp.concatenate([own_rows[0], own_rows[1]], axis=-1)
    right_rows = jnp.concatenate([own_rows[1], -own_rows[0]], axis=-1)
    summed = packed_rows(left_rows, right_rows, left_all, row_start) * frame_scale
    return summed.astype(jnp.bfloat16)


def order_of(step, mine, coarse):
    if coarse == 4:
        high = (mine // 2 + 1 - step // 2) % 2
        low = (mine % 2 + (step + 1) // 2) % 2
        return 2 * high + low
    return (mine + step + 1) % coarse


def filter_rows(fine_count, tap_count, group):
    length = tap_count * fine_count
    offsets = np.arange(length, dtype=np.float64)
    shifted = (offsets - length / 2 + 0.5) / fine_count
    taper = 0.5 - 0.5 * np.cos(2.0 * np.pi * (offsets + 0.5) / length)
    window = np.sinc(shifted) * taper
    window = window / np.sqrt(np.sum(window * window))
    fine = np.arange(fine_count)
    angles = 2.0 * np.pi * ((offsets[None, :] * fine[:, None]) % fine_count) / fine_count
    hcos = window[None, :] * np.cos(angles)
    hsin = window[None, :] * np.sin(angles)
    span = group * fine_count + length
    rows = np.zeros((group, 2, fine_count, 2, span), np.float64)
    for frame in range(group):
        at = slice(frame * fine_count, frame * fine_count + length)
        rows[frame, 0, :, 0, at] = hcos
        rows[frame, 0, :, 1, at] = hsin
        rows[frame, 1, :, 0, at] = -hsin
        rows[frame, 1, :, 1, at] = hcos
    rows = rows.reshape(group * 2 * fine_count, 2 * span).astype(np.float32)
    high = rows.astype(jnp.bfloat16)
    low = (rows - high.astype(np.float32)).astype(jnp.bfloat16)
    return high, low


def products(dims, span, bbuf, turned, obuf):
    ranks, _, _, _, local_inputs, frames, scale = dims
    rows = ranks * local_inputs // 2
    own_sources = ranks // 2
    depth = 2 * frames

    def turn_over(index, part):
        @pl.loop(0, own_sources)
        def _(source):
            at = pl.multiple_of(source * local_inputs, local_inputs)
            where_real = pl.ds(pl.multiple_of(part * frames, frames), frames)
            where_imag = pl.ds(pl.multiple_of(depth + part * frames, frames), frames)
            real = bbuf[index, part, span * own_sources + source, 0].T
            imag = bbuf[index, part, span * own_sources + source, 1].T
            turned[0, pl.ds(at, local_inputs), where_real] = real
            turned[0, pl.ds(at, local_inputs), where_imag] = imag
            turned[1, pl.ds(at, local_inputs), where_real] = imag
            turned[1, pl.ds(at, local_inputs), where_imag] = -real

    width = 2 * local_inputs

    def columns_of(index, pair):
        columns = []
        for side in range(2):
            source = pair * 2 + side
            columns.append(
                jnp.concatenate(
                    [bbuf[index, part, source, piece] for piece in range(2) for part in range(2)],
                    axis=0,
                )
            )
        return jnp.concatenate(columns, axis=1)

    def multiply(index):
        @pl.loop(0, ranks // 4)
        def _(step):
            pair = (1 - span) * (ranks // 4) + step
            block = columns_of(index, pair)
            value = jnp.dot(turned[span], block, preferred_element_type=jnp.float32) * scale
            at = pl.multiple_of(pair * width, width)
            obuf[index, :, pl.ds(at, width)] = value.astype(jnp.bfloat16)

        @pl.loop(0, ranks // 4)
        def _(step):
            pair = span * (ranks // 4) + step
            block = columns_of(index, pair)
            real = jnp.dot(turned[0], block, preferred_element_type=jnp.float32)
            imag = jnp.dot(turned[1], block, preferred_element_type=jnp.float32)
            row = lax.broadcasted_iota(jnp.int32, (rows, width), 0)
            column = step * width + lax.broadcasted_iota(jnp.int32, (rows, width), 1)
            value = jnp.where(row <= column, real, imag) * scale
            at = pl.multiple_of(pair * width, width)
            obuf[index, :, pl.ds(at, width)] = value.astype(jnp.bfloat16)

    return turn_over, multiply


def finish_kernel(dims, part_vis, recv, vis, kept, bbuf, turned, obuf, insem, outsem, bsem, osem):
    chunks, each = dims[2], dims[3]
    late = min(2, chunks - 1)
    first = chunks - late
    span = lax.axis_index("span")
    turn_over, multiply = products(dims, span, bbuf, turned, obuf)

    def fetch(slot, part):
        return pltpu.make_async_copy(
            recv.at[part, first + slot // each, :, slot % each], bbuf.at[slot, part], bsem.at[slot, part]
        )

    def take(channel):
        return pltpu.make_async_copy(part_vis.at[channel], kept.at[channel], insem.at[channel])

    def give(channel):
        return pltpu.make_async_copy(kept.at[channel], vis.at[channel], outsem.at[channel])

    def result(slot):
        return pltpu.make_async_copy(obuf.at[slot], vis.at[first * each + slot], osem.at[slot])

    for part in range(2):
        fetch(0, part).start()
    for channel in range(first * each):
        take(channel).start()
    for slot in range(1, late * each):
        for part in range(2):
            fetch(slot, part).start()
    for slot in range(late * each):
        for part in range(2):
            fetch(slot, part).wait()
            turn_over(slot, part)
        multiply(slot)
        result(slot).start()
        if slot == 0:
            for channel in range(first * each):
                take(channel).wait()
                give(channel).start()
    for slot in range(late * each):
        result(slot).wait()
    for channel in range(first * each):
        give(channel).wait()


def fused_kernel(
    dims, volt, gains, high, low, vis, send, recv,
    xbuf, tbuf, stage, bbuf, turned, obuf,
    xsem, stsem, ssem, rsem, psend, precv, bsem, osem,
):
    ranks, coarse, chunks, each, local_inputs, frames, scale = dims
    halves = ranks // coarse
    samples = frames * FINE
    rows = ranks * local_inputs // 2
    ahead = min(8, chunks)
    early = min(4, chunks)
    late = min(2, chunks - 1)
    beam = lax.axis_index("beam")
    me = lax.axis_index("inp")
    span = lax.axis_index("span")
    mine = me // halves
    my_half = me % halves

    def peer(step, turn):
        return order_of(step, mine, coarse) * halves + (my_half + turn) % halves

    peers = [(step, turn) for step in range(coarse) for turn in range(halves)]
    peers = [pair for pair in peers if pair != (coarse - 1, 0)]

    barrier = pltpu.get_barrier_semaphore()
    for step, turn in peers:
        pl.semaphore_signal(barrier, inc=1, device_id=(beam, peer(step, turn), span), device_id_type=MESH)
    pl.semaphore_signal(barrier, inc=1, device_id=(beam, me, 1 - span), device_id_type=MESH)
    pl.semaphore_wait(barrier, len(peers) + 1)

    def load(step, slot):
        block = order_of(step, mine, coarse)
        return pltpu.make_async_copy(
            volt.at[:, block], xbuf.at[slot, :, :, pl.ds(0, samples)], xsem.at[slot]
        )

    def outgoing(step, turn, chunk):
        other = peer(step, turn)
        return pltpu.make_async_remote_copy(
            src_ref=send.at[other, chunk],
            dst_ref=recv.at[span, chunk, me],
            send_sem=ssem.at[chunk, other],
            recv_sem=rsem.at[chunk, me],
            device_id=(beam, other, span),
            device_id_type=MESH,
        )

    def incoming(step, turn, chunk):
        other = peer(step, turn)
        return pltpu.make_async_remote_copy(
            src_ref=send.at[other, chunk],
            dst_ref=recv.at[span, chunk, other],
            send_sem=ssem.at[chunk, other],
            recv_sem=rsem.at[chunk, other],
            device_id=(beam, other, span),
            device_id_type=MESH,
        )

    def forward(chunk):
        return pltpu.make_async_remote_copy(
            src_ref=recv.at[span, chunk],
            dst_ref=recv.at[span, chunk],
            send_sem=psend.at[chunk],
            recv_sem=precv.at[chunk],
            device_id=(beam, me, 1 - span),
            device_id_type=MESH,
        )

    def backward(chunk):
        return pltpu.make_async_remote_copy(
            src_ref=recv.at[1 - span, chunk],
            dst_ref=recv.at[1 - span, chunk],
            send_sem=psend.at[chunk],
            recv_sem=precv.at[chunk],
            device_id=(beam, me, 1 - span),
            device_id_type=MESH,
        )

    tail = jnp.zeros((2, local_inputs, TAPS * FINE), jnp.bfloat16)
    xbuf[0, :, :, pl.ds(samples, TAPS * FINE)] = tail
    xbuf[1, :, :, pl.ds(samples, TAPS * FINE)] = tail

    def channelize(step, slot):
        load(step, slot).wait()

        @pl.loop(0, frames // 8, unroll=2)
        def _(pair):
            base = pl.multiple_of(pair * (8 * FINE), 4 * FINE)
            pieces = []
            for part in range(2):
                at = base + part * 4 * FINE
                at = pl.multiple_of(at, 4 * FINE)
                pieces.append(
                    jnp.concatenate(
                        [xbuf[slot, 0, :, pl.ds(at, 8 * FINE)], xbuf[slot, 1, :, pl.ds(at, 8 * FINE)]],
                        axis=1,
                    )
                )
            both = jnp.concatenate(pieces, axis=0)
            contract = (((1,), (1,)), ((), ()))
            got = lax.dot_general(high[...], both, contract, preferred_element_type=jnp.float32)
            got = got + lax.dot_general(low[...], both, contract, preferred_element_type=jnp.float32)
            at = pl.multiple_of(pair * (16 * FINE), 16 * FINE)
            tbuf[pl.ds(at, 8 * FINE), :] = got[:, :local_inputs]
            tbuf[pl.ds(at + 8 * FINE, 8 * FINE), :] = got[:, local_inputs:]

    def weigh(step, turn):
        block = order_of(step, mine, coarse)
        half = (my_half + turn) % halves

        @pl.loop(0, chunks * each, unroll=2)
        def _(own):
            chunk = own // each
            index = own % each
            fine = half * (chunks * each) + own
            real = tbuf[pl.ds(fine, frames, stride=2 * FINE), :]
            imag = tbuf[pl.ds(FINE + fine, frames, stride=2 * FINE), :]
            gain_real = gains[block, 0, pl.ds(fine, 1), :]
            gain_imag = gains[block, 1, pl.ds(fine, 1), :]
            stage[half, chunk, index, 0] = (real * gain_real - imag * gain_imag).astype(jnp.bfloat16)
            stage[half, chunk, index, 1] = (real * gain_imag + imag * gain_real).astype(jnp.bfloat16)

    def put(step, turn):
        half = (my_half + turn) % halves
        if (step, turn) == (coarse - 1, 0):
            return pltpu.make_async_copy(stage.at[half], recv.at[span, :, me], stsem.at[turn])
        return pltpu.make_async_copy(stage.at[half], send.at[peer(step, turn)], stsem.at[turn])

    load(0, 0).start()
    for step in range(coarse):
        if step + 1 < coarse:
            load(step + 1, (step + 1) % 2).start()
        channelize(step, step % 2)
        for turn in range(halves):
            weigh(step, turn)
            put(step, turn).start()
            put(step, turn).wait()
            if (step, turn) in peers:
                for chunk in range(early):
                    outgoing(step, turn, chunk).start()
    for chunk in range(early, ahead):
        for step, turn in peers:
            outgoing(step, turn, chunk).start()

    def fetch(chunk, index, part):
        return pltpu.make_async_copy(
            recv.at[part, chunk, :, index], bbuf.at[index, part], bsem.at[index, part]
        )

    def result(chunk, index):
        return pltpu.make_async_copy(obuf.at[index], vis.at[chunk * each + index], osem.at[index])

    turn_over, multiply = products(dims, span, bbuf, turned, obuf)

    def correlate(chunk):
        for index in range(each):
            fetch(chunk, index, span).start()
        for index in range(each):
            fetch(chunk, index, span).wait()
            turn_over(index, span)
            if index == 0:
                backward(chunk).wait_recv()
            fetch(chunk, index, 1 - span).start()
            fetch(chunk, index, 1 - span).wait()
            turn_over(index, 1 - span)

            multiply(index)
            result(chunk, index).start()
        for index in range(each):
            result(chunk, index).wait()

    @pl.loop(0, chunks)
    def _(chunk):
        for step, turn in peers:
            incoming(step, turn, chunk).wait_recv()
        forward(chunk).start()

        @pl.when(chunk + ahead < chunks)
        def _():
            for step, turn in peers:
                outgoing(step, turn, chunk + ahead).start()

        @pl.when(chunk < chunks - late)
        def _():
            correlate(chunk)

        @pl.when(chunk >= chunks - late)
        def _():
            backward(chunk).wait_recv()

    @pl.loop(0, chunks)
    def _(chunk):
        for step, turn in peers:
            outgoing(step, turn, chunk).wait_send()
        forward(chunk).wait_send()


def fused(voltages, gains):
    coarse, local_inputs, samples = voltages.shape[1:]
    ranks = lax.axis_size("inp")
    frames = samples // FINE
    halves = ranks // coarse
    owned = FINE // halves
    each = 1
    chunks = owned // each
    rows = ranks * local_inputs // 2
    columns = ranks * local_inputs
    high, low = filter_rows(FINE, TAPS, 4)
    gain_rows = jnp.transpose(gains, (1, 0, 3, 2))
    scale = 1.0 / (2 * frames)
    dims = (ranks, coarse, chunks, each, local_inputs, frames, scale)
    bf16 = jnp.bfloat16
    anywhere = pl.BlockSpec(memory_space=pl.ANY)
    inside = pl.BlockSpec(memory_space=pltpu.VMEM)
    flops = 4 * owned * rows * columns * 4 * frames
    late = min(2, chunks - 1)
    first = (chunks - late) * each
    part_vis, _, recv = pl.pallas_call(
        functools.partial(fused_kernel, dims),
        out_shape=(
            jax.ShapeDtypeStruct((first, rows, columns), bf16),
            jax.ShapeDtypeStruct((ranks, chunks, each, 2, frames, local_inputs), bf16),
            jax.ShapeDtypeStruct((2, chunks, ranks, each, 2, frames, local_inputs), bf16),
        ),
        in_specs=[anywhere, inside, inside, inside],
        out_specs=(anywhere, anywhere, anywhere),
        scratch_shapes=[
            pltpu.VMEM((2, 2, local_inputs, samples + TAPS * FINE), bf16),
            pltpu.VMEM((frames * 2 * FINE, local_inputs), jnp.float32),
            pltpu.VMEM((halves, chunks, each, 2, frames, local_inputs), bf16),
            pltpu.VMEM((each, 2, ranks, 2, frames, local_inputs), bf16),
            pltpu.VMEM((2, rows, 4 * frames), bf16),
            pltpu.VMEM((each, rows, columns), bf16),
            pltpu.SemaphoreType.DMA((2,)),
            pltpu.SemaphoreType.DMA((halves,)),
            pltpu.SemaphoreType.DMA((chunks, ranks)),
            pltpu.SemaphoreType.DMA((chunks, ranks)),
            pltpu.SemaphoreType.DMA((chunks,)),
            pltpu.SemaphoreType.DMA((chunks,)),
            pltpu.SemaphoreType.DMA((each, 2)),
            pltpu.SemaphoreType.DMA((each,)),
        ],
        compiler_params=pltpu.CompilerParams(
            collective_id=0, has_side_effects=True, vmem_limit_bytes=60 * 1024 * 1024
        ),
        cost_estimate=pl.CostEstimate(flops=flops, bytes_accessed=2 * voltages.size * 8, transcendentals=0),
    )(voltages, gain_rows, jnp.asarray(high), jnp.asarray(low))
    slots = late * each
    return pl.pallas_call(
        functools.partial(finish_kernel, dims),
        out_shape=jax.ShapeDtypeStruct((owned, rows, columns), bf16),
        in_specs=[anywhere, anywhere],
        out_specs=anywhere,
        scratch_shapes=[
            pltpu.VMEM((first, rows, columns), bf16),
            pltpu.VMEM((slots, 2, ranks, 2, frames, local_inputs), bf16),
            pltpu.VMEM((2, rows, 4 * frames), bf16),
            pltpu.VMEM((slots, rows, columns), bf16),
            pltpu.SemaphoreType.DMA((first,)),
            pltpu.SemaphoreType.DMA((first,)),
            pltpu.SemaphoreType.DMA((slots, 2)),
            pltpu.SemaphoreType.DMA((slots,)),
        ],
        compiler_params=pltpu.CompilerParams(vmem_limit_bytes=60 * 1024 * 1024),
    )(part_vis, recv)


def chosen(voltages, gains):
    coarse, local_inputs, samples = voltages.shape[1:]
    ranks, spans = lax.axis_size("inp"), lax.axis_size("span")
    fits = (
        spans == 2
        and local_inputs % 128 == 0
        and ranks % coarse == 0
        and ranks % 4 == 0
        and FINE % (ranks // coarse) == 0
        and samples % (16 * FINE) == 0
    )
    return fused(voltages, gains) if fits else local(voltages, gains)


def solution(mesh):
    placed = (P(None, "beam", "inp", "span"), P(None, "beam", "inp", None))
    return jax.shard_map(
        chosen,
        mesh=mesh,
        in_specs=placed,
        out_specs=P(("beam", "inp"), "span", None),
        check_vma=False,
    )
```
